32 devices in a mesh: tile: 8 (over y, x, core), depth: 4 (over z).
Axes of the slice: x: 2, y: 2, z: 4, core: 2. Of those that a mesh axis runs over, the one named last changes fastest.
Arguments:
- samples: bfloat16 [4, 16, 4096, 128], P('depth', None, 'tile'), may hold values from -6 to 6
- opacity: float32 [4, 16, 4096], P('depth', None, 'tile'), may hold values from 0.004 to 0.06
- counts: int32 [4, 4096], P('depth', 'tile'), may hold values from 0 to 16
- depth_order: int32 [8, 4], P('tile'), may hold values from 0 to 3, each once within a row
- target: float32 [4096, 128], P(('tile', 'depth')), may hold values from -6 to 6
- weight_in: bfloat16 [4, 128, 256], P('depth'), may hold values from -0.5 to 0.5
- weight_out: bfloat16 [4, 256, 128], P('depth'), may hold values from -1.5 to 1.5
Outputs:
- pixels: float32 [4096, 128], P(('tile', 'depth'))
- grad_in: float32 [4, 128, 256], P('depth', 'tile')
- grad_out: float32 [4, 256, 128], P('depth', 'tile')
The draws below stay inside these ranges and needn't reach their ends.
Inputs may be any that keep to these rules, and one draw needn't show every extreme that they name: `depth_order`: each row holds every brick rank 0 to 3 once.
All inputs are finite; a program needn't handle non-finite values.
Results may differ from the reference program's by a relative error of at most 0.0025.
Values sent between devices are 32-bit elements; how exact they have to be, the bound alone decides.
No kernel may reach another device: no remote copies, remote signals or barrier semaphores. Data moves between devices by JAX's collectives and lax.ppermute only.
A program may use at most 64 MiB of HBM per device.

```python
import math
import jax
import jax.numpy as jnp
from jax import lax

ENC = 128
HID = 256
FEAT = 128
SAMPLES = 16
RAYS_TILE = 512
TILES = 8
BRICKS = 4
RAYS = 4096


def set_ends(result, own_key, low, top_value):
    longest = result.shape.index(max(result.shape))
    spots = []
    for shift in (0, 1):
        where = [jax.random.randint(jax.random.fold_in(own_key, axis), (), 0, length) for axis, length in enumerate(result.shape)]
        where[longest] = (where[longest] + shift) % result.shape[longest]
        spots.append(tuple(where))
    return result.at[spots[0]].set(low).at[spots[1]].set(top_value)


def shard_levels(own_key, dims, shards, low, largest):
    factor_of, own = 1.0, jax.random.fold_in(own_key, 6)
    for position, blocks in shards:
        steps = jnp.exp(jax.random.uniform(jax.random.fold_in(own, position), (blocks,), jnp.float32, low / len(shards), largest / len(shards)))
        factor_of = factor_of * jnp.repeat(steps, dims[position] // blocks).reshape([-1 if axis == position else 1 for axis in range(len(dims))])
    return factor_of


def scatter_about(key, dims, width, limit, shards=(), dtype=jnp.bfloat16):
    level = shard_levels(key, dims, shards, -0.22, 0.18) if shards else 1.0
    values = jax.random.normal(key, dims, jnp.float32) * width * level
    return jnp.minimum(jnp.maximum(values, -limit), limit).astype(dtype)


def setup_inputs(seed: int = 0) -> dict:
    keys = jax.random.split(jax.random.key(seed), 8)
    samples = scatter_about(keys[0], (BRICKS, SAMPLES, RAYS, ENC), 1.0, 6.0, ((0, 4), (2, 8)))
    opacity = jnp.clip(jnp.exp(math.log(0.06) - 2.70805 * jax.random.uniform(keys[1], (BRICKS, SAMPLES, RAYS), jnp.float32) ** shard_levels(keys[1], (BRICKS, SAMPLES, RAYS), ((0, 4), (2, 8)), -0.2, 0.2)), 0.004, 0.06)
    counts = set_ends(jax.random.randint(keys[2], (BRICKS, RAYS), 0, 17), jax.random.fold_in(keys[2], 1), 0, 16).astype(jnp.int32)
    depth_order = jax.vmap(lambda own: jax.random.permutation(own, BRICKS))(jax.random.split(keys[3], TILES)).reshape((TILES, BRICKS)).astype(jnp.int32)
    target = scatter_about(keys[4], (RAYS, FEAT), 1.0, 6.0, ((0, 32),), jnp.float32)
    weight_in = scatter_about(keys[5], (BRICKS, ENC, HID), ENC ** -0.5, 0.5, ((0, 4),))
    weight_out = scatter_about(keys[6], (BRICKS, HID, FEAT), (HID // 16) ** -0.5, 1.5, ((0, 4),))
    return dict(samples=samples, opacity=opacity, counts=counts, depth_order=depth_order, target=target, weight_in=weight_in, weight_out=weight_out)


def reference(samples, opacity, counts, depth_order, target, weight_in, weight_out):
    slot_index = lax.broadcasted_iota(jnp.int32, opacity.shape, 1)
    living = (slot_index < counts[:, None, :]).astype(jnp.float32)
    kept = 1.0 - opacity * living
    ones_row = jnp.ones((opacity.shape[0], 1, opacity.shape[2]), jnp.float32)
    through = jnp.cumprod(jnp.concatenate([ones_row, kept[:, :-1, :]], axis=1), axis=1)
    contrib = living * opacity * through
    passing = jnp.prod(kept, axis=1)
    tile_of = (jnp.arange(RAYS) // RAYS_TILE).astype(jnp.int32)
    brick_rank = depth_order[tile_of, :].T
    in_front = brick_rank[None, :, :] < brick_rank[:, None, :]
    veiling = jnp.prod(jnp.where(in_front, passing[None, :, :], 1.0), axis=1)

    def forward(packed):
        inputs, share, first, second = packed
        flat = inputs.reshape(SAMPLES * RAYS, ENC)
        before_act = jnp.dot(flat, first, preferred_element_type=jnp.float32)
        hidden = jnp.maximum(before_act, 0.0).astype(jnp.bfloat16)
        radiance = jnp.dot(hidden, second, preferred_element_type=jnp.float32).reshape(SAMPLES, RAYS, FEAT)
        return jnp.sum(share[:, :, None] * radiance, axis=0)

    factor = contrib * veiling[:, None, :]
    terms = lax.map(forward, (samples, factor, weight_in, weight_out))
    pixels = jnp.sum(terms, axis=0)
    pixel_grad = pixels - target

    def backward(packed):
        inputs, share, first, second = packed
        flat = inputs.reshape(SAMPLES * RAYS, ENC)
        before_act = jnp.dot(flat, first, preferred_element_type=jnp.float32)
        hidden = jnp.maximum(before_act, 0.0).astype(jnp.bfloat16)
        feat_grad = (share[:, :, None] * pixel_grad[None, :, :]).astype(jnp.bfloat16).reshape(SAMPLES * RAYS, FEAT)
        out_grad = jnp.dot(hidden.T, feat_grad, preferred_element_type=jnp.float32)
        hidden_grad = jnp.dot(feat_grad, second.T, preferred_element_type=jnp.float32)
        hidden_grad = jnp.where(before_act > 0.0, hidden_grad, 0.0).astype(jnp.bfloat16)
        in_grad = jnp.dot(flat.T, hidden_grad, preferred_element_type=jnp.float32)
        return in_grad, out_grad

    grad_in, grad_out = lax.map(backward, (samples, factor, weight_in, weight_out))
    return pixels, grad_in, grad_out
```

```python
import functools

import jax
import jax.numpy as jnp
from jax import lax
from jax.experimental import pallas as pl
from jax.experimental.pallas import tpu as pltpu
from jax.sharding import PartitionSpec as P

F32, BF16 = jnp.float32, jnp.bfloat16
VMEM = pl.BlockSpec(memory_space=pltpu.VMEM)
SMEM = pl.BlockSpec(memory_space=pltpu.SMEM)
PARAMS = pltpu.CompilerParams(vmem_limit_bytes=24 << 20)


def call(kernel, outs, *args, flops=0):
    return pl.pallas_call(
        kernel,
        out_shape=[jax.ShapeDtypeStruct(s, d) for s, d in outs],
        in_specs=[s for _, s in args],
        out_specs=[VMEM] * len(outs),
        compiler_params=PARAMS,
        cost_estimate=pl.CostEstimate(flops=flops, bytes_accessed=flops // 256, transcendentals=0),
    )(*[a for a, _ in args])


def split(value):
    high = value.astype(BF16)
    return high, (value - high.astype(F32)).astype(BF16)


def dot(a, b):
    return jnp.dot(a, b, preferred_element_type=F32)


def weights_kernel(opacity, counts, columns, passing):
    slots = opacity.shape[0]
    alive = lax.broadcasted_iota(jnp.int32, opacity.shape, 0) < counts[...]
    covered = jnp.where(alive, opacity[...], 0.0)
    kept = 1.0 - covered
    ones = jnp.ones_like(kept)
    through = jnp.concatenate([ones[:1], kept[:-1]], axis=0)
    step = 1
    while step < slots:
        through = through * jnp.concatenate([ones[:step], through[:-step]], axis=0)
        step *= 2
    columns[...] = (covered * through).T
    passing[...] = through[-1:] * kept[-1:]


def forward_kernel(chunks, own, samples, columns, passing, first, second, *outs):
    sent, kept = outs[: len(chunks)], outs[len(chunks) :]
    slots = samples.shape[0]
    for spot, k in enumerate(chunks):
        rows = sent[spot].shape[0] - 8
        chunk = own[0] ^ k
        start = pl.multiple_of(chunk * rows, rows)
        share = columns[pl.ds(start, rows), :]
        total = None
        for s in range(slots):
            active = jnp.maximum(dot(samples[s, pl.ds(start, rows), :], first[...]), 0.0)
            term = active * share[:, s : s + 1]
            total = term if total is None else total + term
        kept[spot][...] = total
        high, low = split(total)
        sent[spot][:rows] = dot(high, second[...]) + dot(low, second[...])
        line = jnp.zeros((1, rows), F32)
        for c in range(passing.shape[1] // rows):
            line = jnp.where(chunk == c, passing[:, c * rows : (c + 1) * rows], line)
        if rows < sent[spot].shape[1]:
            line = jnp.concatenate([line, jnp.zeros((1, sent[spot].shape[1] - rows), F32)], axis=1)
        sent[spot][rows:] = jnp.broadcast_to(line, (8, sent[spot].shape[1]))


def prepare_kernel(own, samples, columns, first, *rest):
    count = len(rest) - 4
    totals, (masked, turned, highs, lows) = rest[:count], rest[count:]
    slots = samples.shape[0]
    for k in range(count):
        rows = totals[k].shape[0]
        start = pl.multiple_of((own[0] ^ k) * rows, rows)
        share = columns[pl.ds(start, rows), :]
        for s in range(slots):
            block = samples[s, pl.ds(start, rows), :]
            active = dot(block, first[...])
            masked[k, s * rows : (s + 1) * rows] = jnp.where(active > 0.0, share[:, s : s + 1], 0.0).astype(BF16)
            turned[k, :, s * rows : (s + 1) * rows] = block.T
        high, low = split(totals[k][...].T)
        highs[k], lows[k] = high, low


def owner_kernel(own, ranks, target, *rest):
    count = (len(rest) - 1) // 2
    given, pixels, grads = rest[:count], rest[count], rest[count + 1 :]
    rows = target.shape[0]
    lines = [given[k][rows : rows + 1, :rows] for k in range(count)]
    rank = [ranks[0, own[0] ^ k] for k in range(count)]
    veils = []
    for k in range(count):
        veil = jnp.ones((1, rows), F32)
        for j in range(count):
            if j != k:
                veil = veil * jnp.where(rank[j] < rank[k], lines[j], 1.0)
        veils.append(veil)
    while len(veils) % 8:
        veils.append(veils[0])
    turned = jnp.concatenate(veils, axis=0).T
    total = None
    for k in range(count):
        term = given[k][:rows] * turned[:, k : k + 1]
        total = term if total is None else total + term
    pixels[...] = total
    slope = total - target[...]
    for k in range(count):
        grads[k][...] = slope * turned[:, k : k + 1]


def backward_terms(chunks, grads, masked, turned, highs, lows, second):
    inner = outer = None
    for spot, k in enumerate(chunks):
        high, low = split(grads[spot][...])
        rows = high.shape[0]
        across = (((1,), (1,)), ((), ()))
        back = lax.dot_general(high, second[...], across, preferred_element_type=F32)
        back = (back + lax.dot_general(low, second[...], across, preferred_element_type=F32)).astype(BF16)
        part = dot(highs[k], high) + dot(highs[k], low) + dot(lows[k], high)
        outer = part if outer is None else outer + part
        group = 2
        wide = jnp.concatenate([back] * group, axis=0)
        for j in range(0, masked.shape[1], group * rows):
            slope = masked[k, j : j + group * rows] * wide
            part = dot(turned[k, :, j : j + group * rows], slope)
            inner = part if inner is None else inner + part
    return inner, outer


def backward_kernel(chunks, masked, turned, highs, lows, second, *rest):
    grads, (inner, outer) = rest[: len(chunks)], rest[-2:]
    inner[...], outer[...] = backward_terms(chunks, grads, masked, turned, highs, lows, second)


def last_kernel(chunks, place, masked, turned, highs, lows, second, early_in, early_out, *rest):
    grads, (keep, send) = rest[: len(chunks)], rest[-2:]
    inner, outer = backward_terms(chunks, grads, masked, turned, highs, lows, second)
    inner, outer = inner + early_in[...], outer + early_out[...]
    pairs, width = keep.shape[0], keep.shape[2]
    few, many = inner.shape[0] // (2 * pairs), outer.shape[0] // (2 * pairs)
    even = place[0] % 2 == 0

    def put(a, at, one, two):
        size = one.shape[0]
        keep[a, at : at + size] = jnp.where(even, one, two)
        send[a, at : at + size] = jnp.where(even, two, one)

    for a in range(pairs):
        at = 0
        for c in range(0, inner.shape[1], width):
            put(a, at, *[inner[(2 * a + p) * few : (2 * a + p + 1) * few, c : c + width] for p in (0, 1)])
            at += few
        put(a, at, *[outer[(2 * a + p) * many : (2 * a + p + 1) * many] for p in (0, 1)])


def pair_kernel(place, keep, came, *outs):
    pair = place[0] // 2
    for k, out in enumerate(outs):
        out[...] = keep[pair ^ k] + came[pair ^ k]


def finish_kernel(*refs):
    given, (inner, outer) = refs[:-2], refs[-2:]
    total = given[0][...]
    for more in given[1:]:
        total = total + more[...]
    few, width = inner.shape[1], total.shape[1]
    for i, c in enumerate(range(0, inner.shape[2], width)):
        inner[0, :, c : c + width] = total[i * few : (i + 1) * few]
    outer[0] = total[few * (inner.shape[2] // width) :]


def per_device(bricks, tiles, samples, opacity, counts, depth_order, target, weight_in, weight_out):
    samples, opacity, weight_in, weight_out = samples[0], opacity[0], weight_in[0], weight_out[0]
    slots, rays, enc = samples.shape
    hid, feat = weight_out.shape
    rows = rays // bricks
    own = lax.axis_index("depth").astype(jnp.int32)[None]
    place = lax.axis_index("tile").astype(jnp.int32)[None]
    partner = lambda value, axis, size, k: lax.ppermute(value, axis, [(i, i ^ k) for i in range(size)])

    columns, passing = call(
        weights_kernel, [((rays, slots), F32), ((1, rays), F32)], (opacity, VMEM), (counts, VMEM)
    )
    order = list(range(bricks))
    out = call(
        functools.partial(forward_kernel, order),
        [((rows + 8, feat), F32)] * bricks + [((rows, hid), F32)] * bricks,
        (own, SMEM), (samples, VMEM), (columns, VMEM), (passing, VMEM), (weight_in, VMEM), (weight_out, VMEM),
        flops=2 * slots * rays * enc * hid,
    )
    sent, totals = out[:bricks], out[bricks:]
    came = [sent[0]] + [partner(sent[k], "depth", bricks, k) for k in range(1, bricks)]
    masked, turned, highs, lows = call(
        prepare_kernel,
        [
            ((bricks, slots * rows, hid), BF16),
            ((bricks, enc, slots * rows), BF16),
            ((bricks, hid, rows), BF16),
            ((bricks, hid, rows), BF16),
        ],
        (own, SMEM), (samples, VMEM), (columns, VMEM), (weight_in, VMEM), *[(t, VMEM) for t in totals],
        flops=2 * slots * rays * enc * hid,
    )
    out = call(
        owner_kernel,
        [((rows, feat), F32)] * (bricks + 1),
        (own, SMEM), (depth_order, SMEM), (target, VMEM), *[(c, VMEM) for c in came],
    )
    pixels, slopes = out[0], out[1:]
    grads = [slopes[0]] + [partner(slopes[k], "depth", bricks, k) for k in range(1, bricks)]
    saved = [(v, VMEM) for v in (masked, turned, highs, lows, weight_out)]
    early = [0]
    early_in, early_out = call(
        functools.partial(backward_kernel, early),
        [((enc, hid), F32), ((hid, feat), F32)],
        *saved, *[(grads[k], VMEM) for k in early],
        flops=2 * slots * rows * enc * hid,
    )
    late = [k for k in range(bricks) if k not in early]
    pairs = tiles // 2
    part = (enc * hid + hid * feat) // (tiles * feat)
    keep, send = call(
        functools.partial(last_kernel, late),
        [((pairs, part, feat), F32)] * 2,
        (place, SMEM), *saved, (early_in, VMEM), (early_out, VMEM), *[(grads[k], VMEM) for k in late],
        flops=2 * slots * rows * enc * hid * len(late),
    )
    other = partner(send, "tile", tiles, 1)
    parts = call(
        pair_kernel, [((part, feat), F32)] * pairs, (place, SMEM), (keep, VMEM), (other, VMEM)
    )
    parts = [parts[0]] + [partner(parts[k], "tile", tiles, 2 * k) for k in range(1, pairs)]
    grad_in, grad_out = call(
        finish_kernel,
        [((1, enc // tiles, hid), F32), ((1, hid // tiles, feat), F32)],
        *[(p, VMEM) for p in parts],
    )
    return pixels, grad_in, grad_out


def solution(mesh):
    bricks, tiles = mesh.shape["depth"], mesh.shape["tile"]
    placed = (
        P("depth", None, "tile", None),
        P("depth", None, "tile"),
        P("depth", "tile"),
        P("tile", None),
        P(("tile", "depth"), None),
        P("depth", None, None),
        P("depth", None, None),
    )
    return jax.shard_map(
        functools.partial(per_device, bricks, tiles),
        mesh=mesh,
        in_specs=placed,
        out_specs=(P(("tile", "depth"), None), P("depth", "tile", None), P("depth", "tile", None)),
        check_vma=False,
    )
```

```python
import functools

import jax
import jax.numpy as jnp
from jax import lax
from jax.experimental import pallas as pl
from jax.experimental.pallas import tpu as pltpu
from jax.sharding import PartitionSpec as P

F32, BF16 = jnp.float32, jnp.bfloat16
VMEM = pl.BlockSpec(memory_space=pltpu.VMEM)
HBM = pl.BlockSpec(memory_space=pltpu.HBM)
SMEM = pl.BlockSpec(memory_space=pltpu.SMEM)


def call(kernel, outs, scalars, hbm, vmem, flops=0, scratch=(), grant=24):
    return pl.pallas_call(
        kernel,
        out_shape=[jax.ShapeDtypeStruct(s, d) for s, d in outs],
        in_specs=[SMEM] * len(scalars) + [HBM] * len(hbm) + [VMEM] * len(vmem),
        out_specs=[VMEM] * len(outs),
        scratch_shapes=scratch,
        compiler_params=pltpu.CompilerParams(vmem_limit_bytes=grant << 20),
        cost_estimate=pl.CostEstimate(flops=flops, bytes_accessed=flops // 256, transcendentals=0),
    )(*scalars, *[pltpu.with_memory_space_constraint(a, pltpu.HBM) for a in hbm], *vmem)


def split(value):
    high = value.astype(BF16)
    return high, (value - high.astype(F32)).astype(BF16)


def dot(a, b):
    return jnp.dot(a, b, preferred_element_type=F32)


def contributions(opacity, counts):
    slots = opacity.shape[0]
    alive = lax.broadcasted_iota(jnp.int32, opacity.shape, 0) < counts
    covered = jnp.where(alive, opacity, 0.0)
    kept = 1.0 - covered
    ones = jnp.ones_like(kept)
    through = jnp.concatenate([ones[:1], kept[:-1]], axis=0)
    step = 1
    while step < slots:
        through = through * jnp.concatenate([ones[:step], through[:-step]], axis=0)
        step *= 2
    return (covered * through).T, through[-1:] * kept[-1:]


def features(k, own, block, columns, passing, first, second, sent, kept):
    slots, rows, _ = block.shape
    chunk = own[0] ^ k
    share = columns[pl.ds(pl.multiple_of(chunk * rows, rows), rows), :]
    total = None
    for s in range(slots):
        term = jnp.maximum(dot(block[s], first[...]), 0.0) * share[:, s : s + 1]
        total = term if total is None else total + term
    kept[...] = total
    high, low = split(total)
    sent[:rows] = dot(high, second[...]) + dot(low, second[...])
    line = jnp.zeros((1, rows), F32)
    for c in range(passing.shape[1] // rows):
        line = jnp.where(chunk == c, passing[:, c * rows : (c + 1) * rows], line)
    if rows < sent.shape[1]:
        line = jnp.concatenate([line, jnp.zeros((1, sent.shape[1] - rows), F32)], axis=1)
    sent[rows:] = jnp.broadcast_to(line, (8, sent.shape[1]))


def load_kernel(chunks, rest, own, opacity, counts, samples, first, second, target, *refs):
    blocks, columns, passing, first_in, second_in, target_in = refs[:6]
    sent, kept = refs[6 : 6 + len(chunks)], refs[6 + len(chunks) : 6 + 2 * len(chunks)]
    opacity_in, counts_in, sems = refs[-3:]
    rows = blocks.shape[2]
    plain = [(opacity, opacity_in), (counts, counts_in), (first, first_in), (second, second_in), (target, target_in)]
    small = [pltpu.make_async_copy(a, b, sems.at[i]) for i, (a, b) in enumerate(plain)]
    large = {}
    for k in chunks + rest:
        start = pl.multiple_of((own[0] ^ k) * rows, rows)
        large[k] = pltpu.make_async_copy(samples.at[:, pl.ds(start, rows), :], blocks.at[k], sems.at[len(plain) + k])
    for copy in small[:3] + [large[k] for k in chunks] + small[3:4] + [large[k] for k in rest] + small[4:]:
        copy.start()
    small[0].wait()
    small[1].wait()
    columns[...], passing[...] = contributions(opacity_in[...], counts_in[...])
    small[2].wait()
    for spot, k in enumerate(chunks):
        large[k].wait()
        if spot == 0:
            small[3].wait()
        features(k, own, blocks.at[k], columns, passing, first_in, second_in, sent[spot], kept[spot])
    for k in rest:
        large[k].wait()
    small[4].wait()


def near_kernel(chunks, own, blocks, columns, passing, first, second, *outs):
    for spot, k in enumerate(chunks):
        sent, kept = outs[spot], outs[len(chunks) + spot]
        features(k, own, blocks.at[k], columns, passing, first, second, sent, kept)


def prepare_kernel(own, blocks, columns, first, *rest):
    count, slots, rows, _ = blocks.shape
    totals, (masked, turned, highs, lows) = rest[:count], rest[count:]
    for k in range(count):
        start = pl.multiple_of((own[0] ^ k) * rows, rows)
        share = columns[pl.ds(start, rows), :]
        for s in range(slots):
            block = blocks[k, s]
            active = dot(block, first[...])
            masked[k, s * rows : (s + 1) * rows] = jnp.where(active > 0.0, share[:, s : s + 1], 0.0).astype(BF16)
            turned[k, :, s * rows : (s + 1) * rows] = block.T
        highs[k], lows[k] = split(totals[k][...].T)


def owner_kernel(own, ranks, target, *rest):
    count = (len(rest) - 1) // 2
    given, pixels, grads = rest[:count], rest[count], rest[count + 1 :]
    rows = target.shape[0]
    lines = [given[k][rows : rows + 1, :rows] for k in range(count)]
    rank = [ranks[0, own[0] ^ k] for k in range(count)]
    veils = []
    for k in range(count):
        veil = jnp.ones((1, rows), F32)
        for j in range(count):
            if j != k:
                veil = veil * jnp.where(rank[j] < rank[k], lines[j], 1.0)
        veils.append(veil)
    while len(veils) % 8:
        veils.append(veils[0])
    turned = jnp.concatenate(veils, axis=0).T
    total = None
    for k in range(count):
        term = given[k][:rows] * turned[:, k : k + 1]
        total = term if total is None else total + term
    pixels[...] = total
    slope = total - target[...]
    for k in range(count):
        grads[k][...] = slope * turned[:, k : k + 1]


def backward_terms(chunks, grads, masked, turned, highs, lows, second):
    inner = outer = None
    for spot, k in enumerate(chunks):
        high, low = split(grads[spot][...])
        rows = high.shape[0]
        across = (((1,), (1,)), ((), ()))
        back = lax.dot_general(high, second[...], across, preferred_element_type=F32)
        back = (back + lax.dot_general(low, second[...], across, preferred_element_type=F32)).astype(BF16)
        part = dot(highs[k], high) + dot(highs[k], low) + dot(lows[k], high)
        outer = part if outer is None else outer + part
        group = 2
        wide = jnp.concatenate([back] * group, axis=0)
        for j in range(0, masked.shape[1], group * rows):
            slope = masked[k, j : j + group * rows] * wide
            part = dot(turned[k, :, j : j + group * rows], slope)
            inner = part if inner is None else inner + part
    return inner, outer


def backward_kernel(chunks, masked, turned, highs, lows, second, *rest):
    grads, before, (inner, outer) = rest[: len(chunks)], rest[len(chunks) : -2], rest[-2:]
    one, two = backward_terms(chunks, grads, masked, turned, highs, lows, second)
    inner[...], outer[...] = (one + before[0][...], two + before[1][...]) if before else (one, two)


def store_kernel(value, out):
    out[...] = value[...]


def last_kernel(chunks, place, masked, turned, highs, lows, second, early_in, early_out, *rest):
    grads, (keep, send) = rest[: len(chunks)], rest[-2:]
    inner, outer = backward_terms(chunks, grads, masked, turned, highs, lows, second)
    inner, outer = inner + early_in[...], outer + early_out[...]
    pairs, width = keep.shape[0], keep.shape[2]
    few, many = inner.shape[0] // (2 * pairs), outer.shape[0] // (2 * pairs)
    even = place[0] % 2 == 0

    def put(a, at, one, two):
        size = one.shape[0]
        keep[a, at : at + size] = jnp.where(even, one, two)
        send[a, at : at + size] = jnp.where(even, two, one)

    for a in range(pairs):
        at = 0
        for c in range(0, inner.shape[1], width):
            put(a, at, *[inner[(2 * a + p) * few : (2 * a + p + 1) * few, c : c + width] for p in (0, 1)])
            at += few
        put(a, at, *[outer[(2 * a + p) * many : (2 * a + p + 1) * many] for p in (0, 1)])


def pair_kernel(place, keep, came, *outs):
    pair = place[0] // 2
    for k, out in enumerate(outs):
        out[...] = keep[pair ^ k] + came[pair ^ k]


def finish_kernel(*refs):
    given, (inner, outer) = refs[:-2], refs[-2:]
    total = given[0][...]
    for more in given[1:]:
        total = total + more[...]
    few, width = inner.shape[1], total.shape[1]
    for i, c in enumerate(range(0, inner.shape[2], width)):
        inner[0, :, c : c + width] = total[i * few : (i + 1) * few]
    outer[0] = total[few * (inner.shape[2] // width) :]


def per_device(bricks, tiles, samples, opacity, counts, depth_order, target, weight_in, weight_out):
    return step(bricks, tiles, samples[0], opacity[0], counts, depth_order, target, weight_in[0], weight_out[0])


def partner(value, axis, size, k):
    return lax.ppermute(value, axis, [(i, i ^ k) for i in range(size)])


def step(bricks, tiles, samples, opacity, counts, depth_order, target, weight_in, weight_out):
    slots, rays, enc = samples.shape
    hid, feat = weight_out.shape
    rows = rays // bricks
    own = lax.axis_index("depth").astype(jnp.int32)[None]
    place = lax.axis_index("tile").astype(jnp.int32)[None]
    far = list(range(bricks - 1, bricks // 2 - 1, -1))
    near = list(range(bricks // 2 - 1, -1, -1))
    message, sums = ((rows + 8, feat), F32), ((rows, hid), F32)
    flops = 2 * slots * rows * enc * hid

    out = call(
        functools.partial(load_kernel, far, near),
        [
            ((bricks, slots, rows, enc), BF16),
            ((rays, slots), F32),
            ((1, rays), F32),
            (weight_in.shape, BF16),
            (weight_out.shape, BF16),
            (target.shape, F32),
        ]
        + [message] * len(far)
        + [sums] * len(far),
        [own],
        [opacity, counts, samples, weight_in, weight_out, target],
        [],
        flops=flops * len(far),
        scratch=[
            pltpu.VMEM(opacity.shape, F32),
            pltpu.VMEM(counts.shape, jnp.int32),
            pltpu.SemaphoreType.DMA((5 + bricks,)),
        ],
    )
    blocks, columns, passing, first, second, goal = out[:6]
    sent = dict(zip(far, out[6 : 6 + len(far)]))
    totals = dict(zip(far, out[6 + len(far) :]))
    came = {k: partner(sent[k], "depth", bricks, k) for k in far}
    out = call(
        functools.partial(near_kernel, near),
        [message] * len(near) + [sums] * len(near),
        [own],
        [],
        [blocks, columns, passing, first, second],
        flops=flops * len(near),
    )
    sent.update(zip(near, out[: len(near)]))
    totals.update(zip(near, out[len(near) :]))
    came.update({k: partner(sent[k], "depth", bricks, k) if k else sent[k] for k in near})
    masked, turned, highs, lows = call(
        prepare_kernel,
        [
            ((bricks, slots * rows, hid), BF16),
            ((bricks, enc, slots * rows), BF16),
            ((bricks, hid, rows), BF16),
            ((bricks, hid, rows), BF16),
        ],
        [own],
        [],
        [blocks, columns, first] + [totals[k] for k in range(bricks)],
        flops=flops * bricks,
    )
    out = call(
        owner_kernel,
        [((rows, feat), F32)] * (bricks + 1),
        [own, depth_order],
        [],
        [goal] + [came[k] for k in range(bricks)],
    )
    slopes = dict(enumerate(out[1:]))
    grads = {k: partner(slopes[k], "depth", bricks, k) if k else slopes[k] for k in far + near}
    (pixels,) = call(store_kernel, [((rows, feat), F32)], [], [], [out[0]])

    saved = [masked, turned, highs, lows, second]
    gradients = [((enc, hid), F32), ((hid, feat), F32)]
    before = []
    for k in reversed(near):
        before = call(
            functools.partial(backward_kernel, [k]), gradients, [], [], saved + [grads[k]] + list(before), flops=flops
        )
    pairs = tiles // 2
    part = (enc * hid + hid * feat) // (tiles * feat)
    keep, send = call(
        functools.partial(last_kernel, far),
        [((pairs, part, feat), F32)] * 2,
        [place],
        [],
        saved + list(before) + [grads[k] for k in far],
        flops=flops * len(far),
    )
    other = partner(send, "tile", tiles, 1)
    parts = call(pair_kernel, [((part, feat), F32)] * pairs, [place], [], [keep, other])
    parts = [partner(parts[k], "tile", tiles, 2 * k) if k else parts[k] for k in range(pairs - 1, -1, -1)]
    grad_in, grad_out = call(
        finish_kernel, [((1, enc // tiles, hid), F32), ((1, hid // tiles, feat), F32)], [], [], parts
    )
    return pixels, grad_in, grad_out


def solution(mesh):
    bricks, tiles = mesh.shape["depth"], mesh.shape["tile"]
    placed = (
        P("depth", None, "tile", None),
        P("depth", None, "tile"),
        P("depth", "tile"),
        P("tile", None),
        P(("tile", "depth"), None),
        P("depth", None, None),
        P("depth", None, None),
    )
    return jax.shard_map(
        functools.partial(per_device, bricks, tiles),
        mesh=mesh,
        in_specs=placed,
        out_specs=(P(("tile", "depth"), None), P("depth", "tile", None), P("depth", "tile", None)),
        check_vma=False,
    )
```

```python
import functools

import jax
import jax.numpy as jnp
from jax import lax
from jax.experimental import pallas as pl
from jax.experimental.pallas import tpu as pltpu
from jax.sharding import PartitionSpec as P


F32, BF16 = jnp.float32, jnp.bfloat16
VMEM = pl.BlockSpec(memory_space=pltpu.VMEM)
HBM = pl.BlockSpec(memory_space=pltpu.HBM)


def call(kernel, outs, hbm, vmem, flops=0, scratch=(), grant=24):
    return pl.pallas_call(
        kernel,
        out_shape=[jax.ShapeDtypeStruct(s, d) for s, d in outs],
        in_specs=[HBM] * len(hbm) + [VMEM] * len(vmem),
        out_specs=[VMEM] * len(outs),
        scratch_shapes=scratch,
        compiler_params=pltpu.CompilerParams(vmem_limit_bytes=grant << 20),
        cost_estimate=pl.CostEstimate(flops=flops, bytes_accessed=flops // 256, transcendentals=0),
    )(*[pltpu.with_memory_space_constraint(a, pltpu.HBM) for a in hbm], *vmem)


def split(value):
    high = value.astype(BF16)
    return high, (value - high.astype(F32)).astype(BF16)


def dot(a, b):
    return jnp.dot(a, b, preferred_element_type=F32)


def contributions(opacity, counts):
    slots = opacity.shape[0]
    alive = lax.broadcasted_iota(jnp.int32, opacity.shape, 0) < counts
    covered = jnp.where(alive, opacity, 0.0)
    kept = 1.0 - covered
    ones = jnp.ones_like(kept)
    through = jnp.concatenate([ones[:1], kept[:-1]], axis=0)
    step = 1
    while step < slots:
        through = through * jnp.concatenate([ones[:step], through[:-step]], axis=0)
        step *= 2
    return (covered * through).T, through[-1:] * kept[-1:]


def features(k, block, columns, passing, first, second, sent, kept):
    slots, rows, _ = block.shape
    chunk = lax.axis_index("depth") ^ k
    share = columns[pl.ds(pl.multiple_of(chunk * rows, rows), rows), :]
    total = None
    for s in range(slots):
        term = jnp.maximum(dot(block[s], first[...]), 0.0) * share[:, s : s + 1]
        total = term if total is None else total + term
    kept[...] = total
    high, low = split(total)
    sent[:rows] = dot(high, second[...]) + dot(low, second[...])
    line = jnp.zeros((1, rows), F32)
    for c in range(passing.shape[1] // rows):
        line = jnp.where(chunk == c, passing[:, c * rows : (c + 1) * rows], line)
    if rows < sent.shape[1]:
        line = jnp.concatenate([line, jnp.zeros((1, sent.shape[1] - rows), F32)], axis=1)
    sent[rows:] = jnp.broadcast_to(line, (8, sent.shape[1]))


def load_kernel(chunks, rest, opacity, counts, samples, first, second, target, order, *refs):
    blocks, columns, passing, first_in, second_in, target_in, nearer = refs[:7]
    sent, kept = refs[7 : 7 + len(chunks)], refs[7 + len(chunks) : 7 + 2 * len(chunks)]
    opacity_in, counts_in, order_in, sems = refs[-4:]
    bricks, _, rows, _ = blocks.shape
    own = lax.axis_index("depth")
    plain = [(opacity, opacity_in), (counts, counts_in), (first, first_in), (second, second_in)]
    plain += [(target, target_in), (order, order_in)]
    small = [pltpu.make_async_copy(a, b, sems.at[i]) for i, (a, b) in enumerate(plain)]
    large = {}
    for k in chunks + rest:
        start = pl.multiple_of((own ^ k) * rows, rows)
        large[k] = pltpu.make_async_copy(samples.at[:, pl.ds(start, rows), :], blocks.at[k], sems.at[len(plain) + k])
    for copy in small[:3] + [large[k] for k in chunks] + small[3:4] + [large[k] for k in rest] + small[4:]:
        copy.start()
    small[0].wait()
    small[1].wait()
    columns[...], passing[...] = contributions(opacity_in[...], counts_in[...])
    small[2].wait()
    for spot, k in enumerate(chunks):
        large[k].wait()
        if spot == 0:
            small[3].wait()
        features(k, blocks.at[k], columns, passing, first_in, second_in, sent[spot], kept[spot])
    for k in rest:
        large[k].wait()
    small[4].wait()
    small[5].wait()
    rank = [order_in[0, own ^ k] for k in range(bricks)]
    spot = lax.broadcasted_iota(jnp.int32, nearer.shape[1:], 0)
    for k in range(bricks):
        line = jnp.zeros(nearer.shape[1:], jnp.int32)
        for j in range(bricks):
            line = jnp.where(spot == j, jnp.where(rank[j] < rank[k], 1, 0), line)
        nearer[k] = line


def near_kernel(chunks, blocks, columns, passing, first, second, *outs):
    for spot, k in enumerate(chunks):
        sent, kept = outs[spot], outs[len(chunks) + spot]
        features(k, blocks.at[k], columns, passing, first, second, sent, kept)


def prepare_kernel(blocks, columns, first, *rest):
    count, slots, rows, _ = blocks.shape
    totals, (masked, turned, highs, lows) = rest[:count], rest[count:]
    for k in range(count):
        start = pl.multiple_of((lax.axis_index("depth") ^ k) * rows, rows)
        share = columns[pl.ds(start, rows), :]
        for s in range(slots):
            block = blocks[k, s]
            active = dot(block, first[...])
            masked[k, s * rows : (s + 1) * rows] = jnp.where(active > 0.0, share[:, s : s + 1], 0.0).astype(BF16)
            turned[k, :, s * rows : (s + 1) * rows] = block.T
        highs[k], lows[k] = split(totals[k][...].T)


def owner_kernel(target, nearer, *rest):
    count = (len(rest) - 1) // 2
    given, pixels, grads = rest[:count], rest[count], rest[count + 1 :]
    rows = target.shape[0]
    lines = [given[k][rows : rows + 1, :rows] for k in range(count)]
    veils = []
    for k in range(count):
        veil = jnp.ones((1, rows), F32)
        for j in range(count):
            if j != k:
                veil = veil * jnp.where(nearer[k, j : j + 1, :rows] > 0, lines[j], 1.0)
        veils.append(veil)
    while len(veils) % 8:
        veils.append(veils[0])
    turned = jnp.concatenate(veils, axis=0).T
    total = None
    for k in range(count):
        term = given[k][:rows] * turned[:, k : k + 1]
        total = term if total is None else total + term
    pixels[...] = total
    slope = total - target[...]
    for k in range(count):
        grads[k][...] = slope * turned[:, k : k + 1]


def backward_terms(chunks, grads, masked, turned, highs, lows, second):
    inner, outer = [None, None], None
    for spot, k in enumerate(chunks):
        high, low = split(grads[spot][...])
        rows = high.shape[0]
        across = (((1,), (1,)), ((), ()))
        back = lax.dot_general(high, second[...], across, preferred_element_type=F32)
        back = (back + lax.dot_general(low, second[...], across, preferred_element_type=F32)).astype(BF16)
        part = dot(highs[k], high) + dot(highs[k], low) + dot(lows[k], high)
        outer = part if outer is None else outer + part
        group = 2
        wide = jnp.concatenate([back] * group, axis=0)
        for j in range(0, masked.shape[1], group * rows):
            slope = masked[k, j : j + group * rows] * wide
            part = dot(turned[k, :, j : j + group * rows], slope)
            side = j // (group * rows) % 2
            inner[side] = part if inner[side] is None else inner[side] + part
    return inner[0] + inner[1], outer


def backward_kernel(chunks, masked, turned, highs, lows, second, *rest):
    grads, before, (inner, outer) = rest[: len(chunks)], rest[len(chunks) : -2], rest[-2:]
    one, two = backward_terms(chunks, grads, masked, turned, highs, lows, second)
    inner[...], outer[...] = (one + before[0][...], two + before[1][...]) if before else (one, two)


def store_kernel(value, out):
    out[...] = value[...]


def last_kernel(chunks, masked, turned, highs, lows, second, early_in, early_out, *rest):
    grads, (keep, send) = rest[: len(chunks)], rest[-2:]
    inner, outer = backward_terms(chunks, grads, masked, turned, highs, lows, second)
    inner, outer = inner + early_in[...], outer + early_out[...]
    pairs, width = keep.shape[0], keep.shape[2]
    few, many = inner.shape[0] // (2 * pairs), outer.shape[0] // (2 * pairs)
    even = lax.axis_index("tile") % 2 == 0

    def put(a, at, one, two):
        size = one.shape[0]
        keep[a, at : at + size] = jnp.where(even, one, two)
        send[a, at : at + size] = jnp.where(even, two, one)

    for a in range(pairs):
        at = 0
        for c in range(0, inner.shape[1], width):
            put(a, at, *[inner[(2 * a + p) * few : (2 * a + p + 1) * few, c : c + width] for p in (0, 1)])
            at += few
        put(a, at, *[outer[(2 * a + p) * many : (2 * a + p + 1) * many] for p in (0, 1)])


def pair_kernel(keep, came, *outs):
    pair = lax.axis_index("tile") // 2
    for k, out in enumerate(outs):
        out[...] = keep[pair ^ k] + came[pair ^ k]


def finish_kernel(*refs):
    given, (inner, outer) = refs[:-2], refs[-2:]
    total = given[0][...]
    for more in given[1:]:
        total = total + more[...]
    few, width = inner.shape[1], total.shape[1]
    for i, c in enumerate(range(0, inner.shape[2], width)):
        inner[0, :, c : c + width] = total[i * few : (i + 1) * few]
    outer[0] = total[few * (inner.shape[2] // width) :]


def per_device(bricks, tiles, samples, opacity, counts, depth_order, target, weight_in, weight_out):
    return step(bricks, tiles, samples[0], opacity[0], counts, depth_order, target, weight_in[0], weight_out[0])


def partner(value, axis, size, k):
    return lax.ppermute(value, axis, [(i, i ^ k) for i in range(size)])


def step(bricks, tiles, samples, opacity, counts, depth_order, target, weight_in, weight_out):
    slots, rays, enc = samples.shape
    hid, feat = weight_out.shape
    rows = rays // bricks
    far = list(range(bricks // 2, bricks))
    near = list(range(bricks // 2 - 1, -1, -1))
    message, sums = ((rows + 8, feat), F32), ((rows, hid), F32)
    flops = 2 * slots * rows * enc * hid

    out = call(
        functools.partial(load_kernel, far[:1], far[1:] + near),
        [
            ((bricks, slots, rows, enc), BF16),
            ((rays, slots), F32),
            ((1, rays), F32),
            (weight_in.shape, BF16),
            (weight_out.shape, BF16),
            (target.shape, F32),
            ((bricks, -(-bricks // 8) * 8, 128), jnp.int32),
            message,
            sums,
        ],
        [opacity, counts, samples, weight_in, weight_out, target, depth_order],
        [],
        flops=flops,
        scratch=[
            pltpu.VMEM(opacity.shape, F32),
            pltpu.VMEM(counts.shape, jnp.int32),
            pltpu.SMEM(depth_order.shape, jnp.int32),
            pltpu.SemaphoreType.DMA((6 + bricks,)),
        ],
    )
    blocks, columns, passing, first, second, goal, nearer = out[:7]
    sent, totals, came = {far[0]: out[7]}, {far[0]: out[8]}, {}

    def forward(chunks):
        out = call(
            functools.partial(near_kernel, chunks),
            [message] * len(chunks) + [sums] * len(chunks),
            [],
            [blocks, columns, passing, first, second],
            flops=flops * len(chunks),
        )
        sent.update(zip(chunks, out[: len(chunks)]))
        totals.update(zip(chunks, out[len(chunks) :]))

    forward(far[1:])
    forward(near)
    for k in far + near:
        came[k] = partner(sent[k], "depth", bricks, k) if k else sent[k]
    masked, turned, highs, lows = call(
        prepare_kernel,
        [
            ((bricks, slots * rows, hid), BF16),
            ((bricks, enc, slots * rows), BF16),
            ((bricks, hid, rows), BF16),
            ((bricks, hid, rows), BF16),
        ],
        [],
        [blocks, columns, first] + [totals[k] for k in range(bricks)],
        flops=flops * bricks,
    )
    out = call(
        owner_kernel, [((rows, feat), F32)] * (bricks + 1), [], [goal, nearer] + [came[k] for k in range(bricks)]
    )
    slopes = dict(enumerate(out[1:]))
    grads = {k: partner(slopes[k], "depth", bricks, k) if k else slopes[k] for k in far + near}
    (pixels,) = call(store_kernel, [((rows, feat), F32)], [], [out[0]])

    saved = [masked, turned, highs, lows, second]
    gradients = [((enc, hid), F32), ((hid, feat), F32)]
    before = []
    turns = [0, far[-1]] + near[:-1] + far[:-1]
    for k in turns[:-1]:
        before = call(
            functools.partial(backward_kernel, [k]), gradients, [], saved + [grads[k]] + list(before), flops=flops
        )
    pairs = tiles // 2
    part = (enc * hid + hid * feat) // (tiles * feat)
    keep, send = call(
        functools.partial(last_kernel, turns[-1:]),
        [((pairs, part, feat), F32)] * 2,
        [],
        saved + list(before) + [grads[turns[-1]]],
        flops=flops,
    )
    other = partner(send, "tile", tiles, 1)
    parts = call(pair_kernel, [((part, feat), F32)] * pairs, [], [keep, other])
    parts = [partner(parts[k], "tile", tiles, 2 * k) if k else parts[k] for k in range(pairs - 1, -1, -1)]
    grad_in, grad_out = call(finish_kernel, [((1, enc // tiles, hid), F32), ((1, hid // tiles, feat), F32)], [], parts)
    return pixels, grad_in, grad_out


def solution(mesh):
    bricks, tiles = mesh.shape["depth"], mesh.shape["tile"]
    placed = (
        P("depth", None, "tile", None),
        P("depth", None, "tile"),
        P("depth", "tile"),
        P("tile", None),
        P(("tile", "depth"), None),
        P("depth", None, None),
        P("depth", None, None),
    )
    return jax.shard_map(
        functools.partial(per_device, bricks, tiles),
        mesh=mesh,
        in_specs=placed,
        out_specs=(P(("tile", "depth"), None), P("depth", "tile", None), P("depth", "tile", None)),
        check_vma=False,
    )
```

```python
import functools

import jax
import jax.numpy as jnp
from jax import lax
from jax.experimental import pallas as pl
from jax.experimental.pallas import tpu as pltpu
from jax.sharding import PartitionSpec as P


F32, BF16 = jnp.float32, jnp.bfloat16
VMEM = pl.BlockSpec(memory_space=pltpu.VMEM)
HBM = pl.BlockSpec(memory_space=pltpu.HBM)


def call(kernel, outs, hbm, vmem, flops=0, scratch=(), grant=24):
    return pl.pallas_call(
        kernel,
        out_shape=[jax.ShapeDtypeStruct(s, d) for s, d in outs],
        in_specs=[HBM] * len(hbm) + [VMEM] * len(vmem),
        out_specs=[VMEM] * len(outs),
        scratch_shapes=scratch,
        compiler_params=pltpu.CompilerParams(vmem_limit_bytes=grant << 20),
        cost_estimate=pl.CostEstimate(flops=flops, bytes_accessed=flops // 256, transcendentals=0),
    )(*[pltpu.with_memory_space_constraint(a, pltpu.HBM) for a in hbm], *vmem)


def split(value):
    high = value.astype(BF16)
    return high, (value - high.astype(F32)).astype(BF16)


def dot(a, b):
    return jnp.dot(a, b, preferred_element_type=F32)


def contributions(opacity, counts):
    slots = opacity.shape[0]
    alive = lax.broadcasted_iota(jnp.int32, opacity.shape, 0) < counts
    covered = jnp.where(alive, opacity, 0.0)
    kept = 1.0 - covered
    ones = jnp.ones_like(kept)
    through = jnp.concatenate([ones[:1], kept[:-1]], axis=0)
    step = 1
    while step < slots:
        through = through * jnp.concatenate([ones[:step], through[:-step]], axis=0)
        step *= 2
    return (covered * through).T, through[-1:] * kept[-1:]


def features(k, block, columns, passing, first, second, sent, kept):
    slots, rows, _ = block.shape
    chunk = lax.axis_index("depth") ^ k
    share = columns[pl.ds(pl.multiple_of(chunk * rows, rows), rows), :]
    total = None
    for s in range(slots):
        term = jnp.maximum(dot(block[s], first[...]), 0.0) * share[:, s : s + 1]
        total = term if total is None else total + term
    kept[...] = total
    high, low = split(total)
    sent[:rows, 0] = dot(high, second[...]) + dot(low, second[...])
    line = jnp.zeros((1, rows), F32)
    for c in range(passing.shape[1] // rows):
        line = jnp.where(chunk == c, passing[:, c * rows : (c + 1) * rows], line)
    if rows < sent.shape[2]:
        line = jnp.concatenate([line, jnp.zeros((1, sent.shape[2] - rows), F32)], axis=1)
    sent[rows] = line


def load_kernel(chunks, rest, opacity, counts, samples, first, second, target, order, *refs):
    blocks, columns, passing, first_in, second_in, target_in, nearer = refs[:7]
    sent, kept = refs[7 : 7 + len(chunks)], refs[7 + len(chunks) : 7 + 2 * len(chunks)]
    opacity_in, counts_in, order_in, sems = refs[-4:]
    bricks, _, rows, _ = blocks.shape
    own = lax.axis_index("depth")
    plain = [(opacity, opacity_in), (counts, counts_in), (first, first_in), (second, second_in)]
    plain += [(target, target_in), (order, order_in)]
    small = [pltpu.make_async_copy(a, b, sems.at[i]) for i, (a, b) in enumerate(plain)]
    large = {}
    for k in chunks + rest:
        start = pl.multiple_of((own ^ k) * rows, rows)
        large[k] = pltpu.make_async_copy(samples.at[:, pl.ds(start, rows), :], blocks.at[k], sems.at[len(plain) + k])
    for copy in small[:3] + [large[k] for k in chunks] + small[3:4] + [large[k] for k in rest] + small[4:]:
        copy.start()
    small[0].wait()
    small[1].wait()
    columns[...], passing[...] = contributions(opacity_in[...], counts_in[...])
    small[2].wait()
    for spot, k in enumerate(chunks):
        large[k].wait()
        if spot == 0:
            small[3].wait()
        features(k, blocks.at[k], columns, passing, first_in, second_in, sent[spot], kept[spot])
    for k in rest:
        large[k].wait()
    small[4].wait()
    small[5].wait()
    rank = [order_in[0, own ^ k] for k in range(bricks)]
    spot = lax.broadcasted_iota(jnp.int32, nearer.shape[1:], 0)
    for k in range(bricks):
        line = jnp.zeros(nearer.shape[1:], jnp.int32)
        for j in range(bricks):
            line = jnp.where(spot == j, jnp.where(rank[j] < rank[k], 1, 0), line)
        nearer[k] = line


def near_kernel(chunks, blocks, columns, passing, first, second, *outs):
    for spot, k in enumerate(chunks):
        sent, kept = outs[spot], outs[len(chunks) + spot]
        features(k, blocks.at[k], columns, passing, first, second, sent, kept)


def prepare_kernel(blocks, columns, first, *rest):
    count, slots, rows, _ = blocks.shape
    totals, (masked, turned, highs, lows) = rest[:count], rest[count:]
    for k in range(count):
        start = pl.multiple_of((lax.axis_index("depth") ^ k) * rows, rows)
        share = columns[pl.ds(start, rows), :]
        for s in range(slots):
            block = blocks[k, s]
            active = dot(block, first[...])
            masked[k, s * rows : (s + 1) * rows] = jnp.where(active > 0.0, share[:, s : s + 1], 0.0).astype(BF16)
            turned[k, :, s * rows : (s + 1) * rows] = block.T
        highs[k], lows[k] = split(totals[k][...].T)


def owner_kernel(target, nearer, *rest):
    count = (len(rest) - 1) // 2
    given, pixels, grads = rest[:count], rest[count], rest[count + 1 :]
    rows = target.shape[0]
    lines = [given[k][rows][:, :rows] for k in range(count)]
    veils = []
    for k in range(count):
        veil = jnp.ones((1, rows), F32)
        for j in range(count):
            if j != k:
                veil = veil * jnp.where(nearer[k, j : j + 1, :rows] > 0, lines[j], 1.0)
        veils.append(veil)
    while len(veils) % 8:
        veils.append(veils[0])
    turned = jnp.concatenate(veils, axis=0).T
    total = None
    for k in range(count):
        term = given[k][:rows, 0] * turned[:, k : k + 1]
        total = term if total is None else total + term
    pixels[...] = total
    slope = total - target[...]
    for k in range(count):
        grads[k][...] = slope * turned[:, k : k + 1]


def backward_terms(chunks, grads, masked, turned, highs, lows, second):
    inner, outer = [None, None], None
    for spot, k in enumerate(chunks):
        high, low = split(grads[spot][...])
        rows = high.shape[0]
        across = (((1,), (1,)), ((), ()))
        both, twice = jnp.concatenate([high, low], axis=1), jnp.concatenate([second[...]] * 2, axis=1)
        back = lax.dot_general(both, twice, across, preferred_element_type=F32).astype(BF16)
        part = dot(highs[k], high) + dot(highs[k], low) + dot(lows[k], high)
        outer = part if outer is None else outer + part
        group = 2
        wide = jnp.concatenate([back] * group, axis=0)
        for j in range(0, masked.shape[1], group * rows):
            slope = masked[k, j : j + group * rows] * wide
            part = dot(turned[k, :, j : j + group * rows], slope)
            side = j // (group * rows) % 2
            inner[side] = part if inner[side] is None else inner[side] + part
    return inner[0] + inner[1], outer


def backward_kernel(chunks, masked, turned, highs, lows, second, *rest):
    grads, before, (inner, outer) = rest[: len(chunks)], rest[len(chunks) : -2], rest[-2:]
    one, two = backward_terms(chunks, grads, masked, turned, highs, lows, second)
    inner[...], outer[...] = (one + before[0][...], two + before[1][...]) if before else (one, two)


def store_kernel(value, out):
    out[...] = value[...]


def last_kernel(chunks, masked, turned, highs, lows, second, early_in, early_out, *rest):
    grads, (keep, send) = rest[: len(chunks)], rest[-2:]
    inner, outer = backward_terms(chunks, grads, masked, turned, highs, lows, second)
    inner, outer = inner + early_in[...], outer + early_out[...]
    pairs, width = keep.shape[0], keep.shape[2]
    few, many = inner.shape[0] // (2 * pairs), outer.shape[0] // (2 * pairs)
    even = lax.axis_index("tile") % 2 == 0

    def put(a, at, one, two):
        size = one.shape[0]
        keep[a, at : at + size] = jnp.where(even, one, two)
        send[a, at : at + size] = jnp.where(even, two, one)

    for a in range(pairs):
        at = 0
        for c in range(0, inner.shape[1], width):
            put(a, at, *[inner[(2 * a + p) * few : (2 * a + p + 1) * few, c : c + width] for p in (0, 1)])
            at += few
        put(a, at, *[outer[(2 * a + p) * many : (2 * a + p + 1) * many] for p in (0, 1)])


def pair_kernel(keep, came, *outs):
    pair = lax.axis_index("tile") // 2
    for k, out in enumerate(outs):
        out[...] = keep[pair ^ k] + came[pair ^ k]


def finish_kernel(*refs):
    given, (inner, outer) = refs[:-2], refs[-2:]
    total = given[0][...]
    for more in given[1:]:
        total = total + more[...]
    few, width = inner.shape[1], total.shape[1]
    for i, c in enumerate(range(0, inner.shape[2], width)):
        inner[0, :, c : c + width] = total[i * few : (i + 1) * few]
    outer[0] = total[few * (inner.shape[2] // width) :]


def per_device(bricks, tiles, samples, opacity, counts, depth_order, target, weight_in, weight_out):
    return step(bricks, tiles, samples[0], opacity[0], counts, depth_order, target, weight_in[0], weight_out[0])


def partner(value, axis, size, k):
    return lax.ppermute(value, axis, [(i, i ^ k) for i in range(size)])


def step(bricks, tiles, samples, opacity, counts, depth_order, target, weight_in, weight_out):
    slots, rays, enc = samples.shape
    hid, feat = weight_out.shape
    rows = rays // bricks
    far = list(range(bricks // 2, bricks))
    near = list(range(bricks // 2 - 1, -1, -1))
    message, sums = ((rows + 1, 1, feat), F32), ((rows, hid), F32)
    flops = 2 * slots * rows * enc * hid

    out = call(
        functools.partial(load_kernel, far[:1], far[1:] + near),
        [
            ((bricks, slots, rows, enc), BF16),
            ((rays, slots), F32),
            ((1, rays), F32),
            (weight_in.shape, BF16),
            (weight_out.shape, BF16),
            (target.shape, F32),
            ((bricks, -(-bricks // 8) * 8, 128), jnp.int32),
            message,
            sums,
        ],
        [opacity, counts, samples, weight_in, weight_out, target, depth_order],
        [],
        flops=flops,
        scratch=[
            pltpu.VMEM(opacity.shape, F32),
            pltpu.VMEM(counts.shape, jnp.int32),
            pltpu.SMEM(depth_order.shape, jnp.int32),
            pltpu.SemaphoreType.DMA((6 + bricks,)),
        ],
    )
    blocks, columns, passing, first, second, goal, nearer = out[:7]
    sent, totals, came = {far[0]: out[7]}, {far[0]: out[8]}, {}

    def forward(chunks):
        out = call(
            functools.partial(near_kernel, chunks),
            [message] * len(chunks) + [sums] * len(chunks),
            [],
            [blocks, columns, passing, first, second],
            flops=flops * len(chunks),
        )
        sent.update(zip(chunks, out[: len(chunks)]))
        totals.update(zip(chunks, out[len(chunks) :]))

    forward(far[1:])
    forward(near)
    for k in far + near:
        came[k] = partner(sent[k], "depth", bricks, k) if k else sent[k]
    masked, turned, highs, lows = call(
        prepare_kernel,
        [
            ((bricks, slots * rows, hid), BF16),
            ((bricks, enc, slots * rows), BF16),
            ((bricks, hid, rows), BF16),
            ((bricks, hid, rows), BF16),
        ],
        [],
        [blocks, columns, first] + [totals[k] for k in range(bricks)],
        flops=flops * bricks,
    )
    out = call(
        owner_kernel, [((rows, feat), F32)] * (bricks + 1), [], [goal, nearer] + [came[k] for k in range(bricks)]
    )
    slopes = dict(enumerate(out[1:]))
    grads = {k: partner(slopes[k], "depth", bricks, k) if k else slopes[k] for k in far + near}
    (pixels,) = call(store_kernel, [((rows, feat), F32)], [], [out[0]])

    saved = [masked, turned, highs, lows, second]
    gradients = [((enc, hid), F32), ((hid, feat), F32)]
    before = []
    turns = [0, far[-1]] + near[:-1] + far[:-1]
    for k in turns[:-1]:
        before = call(
            functools.partial(backward_kernel, [k]), gradients, [], saved + [grads[k]] + list(before), flops=flops
        )
    pairs = tiles // 2
    part = (enc * hid + hid * feat) // (tiles * feat)
    keep, send = call(
        functools.partial(last_kernel, turns[-1:]),
        [((pairs, part, feat), F32)] * 2,
        [],
        saved + list(before) + [grads[turns[-1]]],
        flops=flops,
    )
    other = partner(send, "tile", tiles, 1)
    parts = call(pair_kernel, [((part, feat), F32)] * pairs, [], [keep, other])
    parts = [partner(parts[k], "tile", tiles, 2 * k) if k else parts[k] for k in range(pairs - 1, -1, -1)]
    grad_in, grad_out = call(finish_kernel, [((1, enc // tiles, hid), F32), ((1, hid // tiles, feat), F32)], [], parts)
    return pixels, grad_in, grad_out


def solution(mesh):
    bricks, tiles = mesh.shape["depth"], mesh.shape["tile"]
    placed = (
        P("depth", None, "tile", None),
        P("depth", None, "tile"),
        P("depth", "tile"),
        P("tile", None),
        P(("tile", "depth"), None),
        P("depth", None, None),
        P("depth", None, None),
    )
    return jax.shard_map(
        functools.partial(per_device, bricks, tiles),
        mesh=mesh,
        in_specs=placed,
        out_specs=(P(("tile", "depth"), None), P("depth", "tile", None), P("depth", "tile", None)),
        check_vma=False,
    )
```
